32 devices in a mesh: shift: 2 (over y), row: 8 (over z, x), col: 2 (over core).
Axes of the slice: x: 2, y: 2, z: 4, core: 2. Of those that a mesh axis runs over, the one named last changes fastest.
Arguments:
- krylov_basis: float32 [128, 3, 8, 8, 128], P('shift', None, 'row', 'col'), parts along dimension 0, may hold values from -4000 to 4000, as said below
- regions: int32 [8, 8, 128], P('row', 'col'), may hold values from 0 to 7
- mu_table: float32 [8], replicated, may hold values from 0.5 to 2
- eps_table: float32 [8], replicated, may hold values from 1 to 4
- shift_value: float32 [2], P('shift'), parts along dimension 0, may hold values from 0.5 to 2
Outputs:
- orthonormal: float32 [128, 3, 8, 8, 128], P('shift', None, 'row', 'col'), parts along dimension 0
- upper_factor: float32 [128, 64], P('shift'), parts along dimension 0
- applied: float32 [128, 3, 8, 8, 128], P('shift', None, 'row', 'col'), parts along dimension 0
- projected: float32 [128, 64], P('shift'), parts along dimension 0
The draws below stay inside these ranges and needn't reach their ends.
There are 2 independent parts, one for each index of `shift`. The reference program is written for one: setup_inputs(seed, part) draws one part's arguments, and reference() takes and returns one part's arrays. A program takes and returns all parts, laid end to end along the dimension named above; an argument that names none is the same for every part. Nothing has to cross between parts.
Inputs may be any that keep to these rules, and one draw needn't show every extreme that they name: `krylov_basis`: Real-valued entries.
All inputs are finite; a program needn't handle non-finite values.
Results may differ from the reference program's by a relative error of at most 0.000071.
Values sent between devices are 32-bit elements; how exact they have to be, the bound alone decides.
A program may use at most 64 MiB of HBM per device.

```python
import math
import jax
import jax.numpy as jnp
from jax import lax

COLS = 64
NZ = 128
NREG = 8
NX = 8
NY = 8


def draw_krylov_basis(key, part):
    keys = jax.random.split(jax.random.fold_in(key, 71), 3)
    normals = jnp.clip(jax.random.normal(keys[0], (COLS, 3, NX, NY, NZ), jnp.float32), -5.0, 5.0)
    position = jnp.arange(NX, dtype=jnp.float32) / max(NX - 1, 1)
    along_x = 1.0 + 2.0 * position
    column_scale = jnp.exp(jax.random.uniform(keys[1], (COLS,), jnp.float32) * jnp.log(10.0))
    cell_scale = jnp.exp(jax.random.uniform(keys[2], (3, NX, NY, NZ), jnp.float32) * jnp.log(3.0))
    scaled = normals * column_scale[:, None, None, None, None]
    scaled = scaled * along_x[None, None, :, None, None] * cell_scale[None]
    return scaled.astype(jnp.float32)


def set_ends(entries, stream_key, low, high):
    longest = entries.shape.index(max(entries.shape))
    spots = []
    for shift in (0, 1):
        where = [jax.random.randint(jax.random.fold_in(stream_key, axis), (), 0, length) for axis, length in enumerate(entries.shape)]
        where[longest] = (where[longest] + shift) % entries.shape[longest]
        spots.append(tuple(where))
    return entries.at[spots[0]].set(low).at[spots[1]].set(high)


def setup_inputs(seed: int = 0, part: int = 0) -> dict:
    streams_of = jax.random.split(jax.random.key(seed), 6)
    part_keys = jax.random.split(jax.random.fold_in(streams_of[5], part), 6)
    return {
        "krylov_basis": draw_krylov_basis(jax.random.fold_in(jax.random.fold_in(streams_of[5], part), 71), part),
        "regions": set_ends(jax.random.randint(streams_of[1], (NX, NY, NZ), 0, NREG), jax.random.fold_in(streams_of[1], 1), 0, NREG - 1).astype(jnp.int32),
        "mu_table": jnp.clip(jnp.exp(jax.random.uniform(streams_of[2], (NREG,), jnp.float32, math.log(0.5), math.log(2.0))), 0.5, 2.0),
        "eps_table": jnp.clip(jnp.exp(jax.random.uniform(streams_of[3], (NREG,), jnp.float32, math.log(1.0), math.log(4.0))), 1.0, 4.0),
        "shift_value": jnp.clip(jax.random.uniform(part_keys[4], (1,), jnp.float32, 0.5, 2.0), 0.5, 2.0),
    }


def forward_z(values):
    return jnp.pad(values[..., 1:], ((0, 0), (0, 0), (0, 0), (0, 1))) - values

def backward_z(values):
    return values - jnp.pad(values[..., :-1], ((0, 0), (0, 0), (0, 0), (1, 0)))

def operator_block(padded_field, coupling, permittivity, shift_scalar):
    cells_x = padded_field.shape[2] - 2
    cells_y = padded_field.shape[3] - 2
    field_x = padded_field[:, 0]
    field_y = padded_field[:, 1]
    field_z = padded_field[:, 2]

    def corner_part(values):
        return values[:, :cells_x + 1, :cells_y + 1]

    def forward_x(values):
        return values[:, 1:cells_x + 2, :cells_y + 1] - corner_part(values)

    def forward_y(values):
        return values[:, :cells_x + 1, 1:cells_y + 2] - corner_part(values)

    def forward_dz(values):
        return forward_z(corner_part(values))
    curl_x = forward_y(field_z) - forward_dz(field_y)
    curl_y = forward_dz(field_x) - forward_x(field_z)
    curl_z = forward_x(field_y) - forward_y(field_x)
    weighted_x = coupling * curl_x
    weighted_y = coupling * curl_y
    weighted_z = coupling * curl_z

    def backward_x(values):
        return values[:, 1:, 1:] - values[:, :-1, 1:]

    def backward_y(values):
        return values[:, 1:, 1:] - values[:, 1:, :-1]

    def backward_dz(values):
        return backward_z(values[:, 1:, 1:])
    result_x = backward_y(weighted_z) - backward_dz(weighted_y)
    result_y = backward_dz(weighted_x) - backward_x(weighted_z)
    result_z = backward_x(weighted_y) - backward_y(weighted_x)
    interior = padded_field[:, :, 1:cells_x + 1, 1:cells_y + 1]
    stacked = jnp.stack([result_x, result_y, result_z], axis=1)
    return stacked - shift_scalar * permittivity * interior

def reference(krylov_basis, regions, mu_table, eps_table, shift_value):
    total_rows = 3 * NX * NY * NZ
    flattened = krylov_basis.reshape(COLS, -1)
    gram_matrix = jnp.dot(flattened.astype(jnp.float32), flattened.T.astype(jnp.float32), precision=lax.Precision.HIGHEST, preferred_element_type=jnp.float32) / total_rows
    lower_factor = jnp.linalg.cholesky(gram_matrix)
    upper_factor = lower_factor.T
    inverse = lax.linalg.triangular_solve(lower_factor, jnp.eye(COLS, dtype=jnp.float32), left_side=True, lower=True)
    ortho_flat = jnp.dot(inverse.astype(jnp.float32), flattened.astype(jnp.float32), precision=lax.Precision.HIGHEST, preferred_element_type=jnp.float32)
    orthonormal = ortho_flat.reshape(krylov_basis.shape)
    coupling = jnp.pad(mu_table[regions], ((1, 0), (1, 0), (0, 0)))
    permittivity = eps_table[regions]
    shift_scalar = shift_value[0]
    blocks = orthonormal.reshape((COLS // 8, 8) + krylov_basis.shape[1:])

    def apply_block(column_block):
        padded_field = jnp.pad(column_block, ((0, 0), (0, 0), (1, 1), (1, 1), (0, 0)))
        return operator_block(padded_field, coupling, permittivity, shift_scalar)
    applied = lax.map(apply_block, blocks).reshape(krylov_basis.shape)
    projected = jnp.dot(ortho_flat.astype(jnp.float32), applied.reshape(COLS, -1).T.astype(jnp.float32), precision=lax.Precision.HIGHEST, preferred_element_type=jnp.float32) / total_rows
    return (orthonormal, upper_factor, applied, projected)
```

```python
import jax
import jax.numpy as jnp
from jax import lax
from jax.sharding import PartitionSpec as P


def shifted(x, axis, by):
    peers = lax.axis_size(axis)
    pairs = [(i, i + by) for i in range(peers) if 0 <= i + by < peers]
    return lax.ppermute(x, axis, pairs)


def padded(x, sides, width):
    for axis, dim in sides:
        peers, length = (lax.axis_size(axis), x.shape[dim])
        up = [(i, (i + 1) % peers) for i in range(peers - 1)]
        down = [(j, i) for i, j in up]
        last = lax.slice_in_dim(x, length - width, length, axis=dim)
        leading = lax.slice_in_dim(x, 0, width, axis=dim)
        before = lax.ppermute(last, axis, up)
        after = lax.ppermute(leading, axis, down)
        x = jnp.concatenate([before, x, after], axis=dim)
    return x


def forward_z(values):
    return jnp.pad(values[..., 1:], ((0, 0), (0, 0), (0, 0), (0, 1))) - values


def backward_z(values):
    return values - jnp.pad(values[..., :-1], ((0, 0), (0, 0), (0, 0), (1, 0)))


def operator_block(padded_field, coupling, permittivity, shift_scalar):
    cells_x = padded_field.shape[2] - 2
    cells_y = padded_field.shape[3] - 2
    field_x = padded_field[:, 0]
    field_y = padded_field[:, 1]
    field_z = padded_field[:, 2]

    def corner_part(values):
        return values[:, : cells_x + 1, : cells_y + 1]

    def forward_x(values):
        return values[:, 1 : cells_x + 2, : cells_y + 1] - corner_part(values)

    def forward_y(values):
        return values[:, : cells_x + 1, 1 : cells_y + 2] - corner_part(values)

    def forward_dz(values):
        return forward_z(corner_part(values))

    curl_x = forward_y(field_z) - forward_dz(field_y)
    curl_y = forward_dz(field_x) - forward_x(field_z)
    curl_z = forward_x(field_y) - forward_y(field_x)
    weighted_x = coupling * curl_x
    weighted_y = coupling * curl_y
    weighted_z = coupling * curl_z

    def backward_x(values):
        return values[:, 1:, 1:] - values[:, :-1, 1:]

    def backward_y(values):
        return values[:, 1:, 1:] - values[:, 1:, :-1]

    def backward_dz(values):
        return backward_z(values[:, 1:, 1:])

    result_x = backward_y(weighted_z) - backward_dz(weighted_y)
    result_y = backward_dz(weighted_x) - backward_x(weighted_z)
    result_z = backward_x(weighted_y) - backward_y(weighted_x)
    interior = padded_field[:, :, 1 : cells_x + 1, 1 : cells_y + 1]
    stacked = jnp.stack([result_x, result_y, result_z], axis=1)
    return stacked - shift_scalar * permittivity * interior


def lookup(labels, table):
    result = jnp.zeros(labels.shape, jnp.float32)
    for region in range(table.shape[0]):
        result = result + jnp.where(labels == region, table[region], 0.0)
    return result


def inner_products(left, right):
    return jnp.dot(
        left, right.T, precision=lax.Precision.HIGHEST, preferred_element_type=jnp.float32
    )


def apply_operator(padded_basis, coupling, permittivity, shift_scalar):
    columns = padded_basis.shape[0]
    blocks = padded_basis.reshape((columns // 16, 16) + padded_basis.shape[1:])

    def apply_block(column_block):
        return operator_block(column_block, coupling, permittivity, shift_scalar)

    images = lax.map(apply_block, blocks)
    return images.reshape((columns,) + images.shape[2:])


def factor_inverse(gram_matrix):
    lower_factor = jnp.linalg.cholesky(gram_matrix)
    inverse = lax.linalg.triangular_solve(
        lower_factor, jnp.eye(gram_matrix.shape[0], dtype=jnp.float32), left_side=True, lower=True
    )
    return (lower_factor.T, inverse)


def local(krylov_basis, regions, mu_table, eps_table, shift_value):
    columns = krylov_basis.shape[0]
    flattened = krylov_basis.reshape(columns, -1)
    total_rows = flattened.shape[1] * lax.axis_size("row") * lax.axis_size("col")
    cells_y = regions.shape[1]
    labels = regions + 1
    from_lower_row = shifted(labels, "row", 1)
    from_lower_col = shifted(labels[:, cells_y - 1 :], "col", 1)
    corner_zero = jnp.zeros((1, 1, labels.shape[2]), jnp.int32)
    top_layer = jnp.concatenate([corner_zero, from_lower_row], axis=1)
    rest_layers = jnp.concatenate([from_lower_col, labels], axis=1)
    padded_ids = jnp.concatenate([top_layer, rest_layers], axis=0)
    mu_extended = jnp.concatenate([jnp.zeros((1,), jnp.float32), mu_table])
    coupling = lookup(padded_ids, mu_extended)
    permittivity = lookup(regions, eps_table)
    shift_scalar = shift_value[0]
    padded_basis = padded(krylov_basis, (("row", 2), ("col", 3)), 1)
    image_basis = apply_operator(padded_basis, coupling, permittivity, shift_scalar)
    image_flat = image_basis.reshape(columns, -1)
    partial = jnp.stack(
        [
            inner_products(flattened, flattened) / total_rows,
            inner_products(flattened, image_flat) / total_rows,
        ]
    )
    gram_matrix, raw_proj = jnp.sum(lax.all_gather(partial, ("row", "col")), axis=0)
    upper_factor, inverse = factor_inverse(gram_matrix)
    orthonormal = jnp.dot(
        inverse, flattened, precision=lax.Precision.HIGHEST, preferred_element_type=jnp.float32
    ).reshape(krylov_basis.shape)
    applied = jnp.dot(
        inverse, image_flat, precision=lax.Precision.HIGHEST, preferred_element_type=jnp.float32
    ).reshape(krylov_basis.shape)
    half_proj = jnp.dot(
        inverse, raw_proj, precision=lax.Precision.HIGHEST, preferred_element_type=jnp.float32
    )
    projected = inner_products(half_proj, inverse)
    return (orthonormal, upper_factor, applied, projected)


def solution(mesh):
    placed = (P("shift", None, "row", "col", None), P("row", "col", None), P(), P(), P("shift"))
    return jax.shard_map(
        local,
        mesh=mesh,
        in_specs=placed,
        out_specs=(
            P("shift", None, "row", "col", None),
            P("shift", None),
            P("shift", None, "row", "col", None),
            P("shift", None),
        ),
        check_vma=False,
    )
```

```python
import jax
import jax.numpy as jnp
from jax import lax
from jax.sharding import PartitionSpec as P


def shifted(x, axis, by):
    peers = lax.axis_size(axis)
    pairs = [(i, i + by) for i in range(peers) if 0 <= i + by < peers]
    return lax.ppermute(x, axis, pairs)


def padded(x, sides, width):
    for axis, dim in sides:
        peers, length = (lax.axis_size(axis), x.shape[dim])
        up = [(i, (i + 1) % peers) for i in range(peers - 1)]
        down = [(j, i) for i, j in up]
        last = lax.slice_in_dim(x, length - width, length, axis=dim)
        leading = lax.slice_in_dim(x, 0, width, axis=dim)
        before = lax.ppermute(last, axis, up)
        after = lax.ppermute(leading, axis, down)
        x = jnp.concatenate([before, x, after], axis=dim)
    return x


def forward_z(values):
    return jnp.pad(values[..., 1:], ((0, 0), (0, 0), (0, 0), (0, 1))) - values


def backward_z(values):
    return values - jnp.pad(values[..., :-1], ((0, 0), (0, 0), (0, 0), (1, 0)))


def operator_block(padded_field, coupling, permittivity, shift_scalar):
    cells_x = padded_field.shape[2] - 2
    cells_y = padded_field.shape[3] - 2
    field_x = padded_field[:, 0]
    field_y = padded_field[:, 1]
    field_z = padded_field[:, 2]

    def corner_part(values):
        return values[:, : cells_x + 1, : cells_y + 1]

    def forward_x(values):
        return values[:, 1 : cells_x + 2, : cells_y + 1] - corner_part(values)

    def forward_y(values):
        return values[:, : cells_x + 1, 1 : cells_y + 2] - corner_part(values)

    def forward_dz(values):
        return forward_z(corner_part(values))

    curl_x = forward_y(field_z) - forward_dz(field_y)
    curl_y = forward_dz(field_x) - forward_x(field_z)
    curl_z = forward_x(field_y) - forward_y(field_x)
    weighted_x = coupling * curl_x
    weighted_y = coupling * curl_y
    weighted_z = coupling * curl_z

    def backward_x(values):
        return values[:, 1:, 1:] - values[:, :-1, 1:]

    def backward_y(values):
        return values[:, 1:, 1:] - values[:, 1:, :-1]

    def backward_dz(values):
        return backward_z(values[:, 1:, 1:])

    result_x = backward_y(weighted_z) - backward_dz(weighted_y)
    result_y = backward_dz(weighted_x) - backward_x(weighted_z)
    result_z = backward_x(weighted_y) - backward_y(weighted_x)
    interior = padded_field[:, :, 1 : cells_x + 1, 1 : cells_y + 1]
    stacked = jnp.stack([result_x, result_y, result_z], axis=1)
    return stacked - shift_scalar * permittivity * interior


def lookup(labels, table):
    regions = jnp.arange(table.shape[0], dtype=labels.dtype)
    chosen = jnp.where(labels[..., None] == regions, table, 0.0)
    return jnp.sum(chosen, axis=-1)


def inner_products(left, right):
    return jnp.dot(
        left, right.T, precision=lax.Precision.HIGHEST, preferred_element_type=jnp.float32
    )


def apply_operator(padded_basis, coupling, permittivity, shift_scalar):
    columns = padded_basis.shape[0]
    blocks = padded_basis.reshape((columns // 16, 16) + padded_basis.shape[1:])

    def apply_block(column_block):
        return operator_block(column_block, coupling, permittivity, shift_scalar)

    images = lax.map(apply_block, blocks)
    return images.reshape((columns,) + images.shape[2:])


def factor_inverse(gram_matrix):
    lower_factor = jnp.linalg.cholesky(gram_matrix)
    inverse = lax.linalg.triangular_solve(
        lower_factor, jnp.eye(gram_matrix.shape[0], dtype=jnp.float32), left_side=True, lower=True
    )
    return (lower_factor.T, inverse)


def local(krylov_basis, regions, mu_table, eps_table, shift_value):
    columns = krylov_basis.shape[0]
    flattened = krylov_basis.reshape(columns, -1)
    total_rows = flattened.shape[1] * lax.axis_size("row") * lax.axis_size("col")
    cells_y = regions.shape[1]
    local_mu = lookup(regions, mu_table)
    from_lower_row = shifted(local_mu, "row", 1)
    from_lower_col = shifted(local_mu[:, cells_y - 1 :], "col", 1)
    corner_zero = jnp.zeros((1, 1, local_mu.shape[2]), jnp.float32)
    top_layer = jnp.concatenate([corner_zero, from_lower_row], axis=1)
    rest_layers = jnp.concatenate([from_lower_col, local_mu], axis=1)
    coupling = jnp.concatenate([top_layer, rest_layers], axis=0)
    permittivity = lookup(regions, eps_table)
    shift_scalar = shift_value[0]
    padded_basis = padded(krylov_basis, (("row", 2), ("col", 3)), 1)
    image_basis = operator_block(padded_basis, coupling, permittivity, shift_scalar)
    image_flat = image_basis.reshape(columns, -1)
    partial = jnp.stack(
        [
            inner_products(flattened, flattened) / total_rows,
            inner_products(flattened, image_flat) / total_rows,
        ]
    )
    gram_matrix, raw_proj = jnp.sum(lax.all_gather(partial, ("row", "col")), axis=0)
    upper_factor, inverse = factor_inverse(gram_matrix)
    orthonormal = jnp.dot(
        inverse, flattened, precision=lax.Precision.HIGHEST, preferred_element_type=jnp.float32
    ).reshape(krylov_basis.shape)
    applied = jnp.dot(
        inverse, image_flat, precision=lax.Precision.HIGHEST, preferred_element_type=jnp.float32
    ).reshape(krylov_basis.shape)
    half_proj = jnp.dot(
        inverse, raw_proj, precision=lax.Precision.HIGHEST, preferred_element_type=jnp.float32
    )
    projected = inner_products(half_proj, inverse)
    return (orthonormal, upper_factor, applied, projected)


def solution(mesh):
    placed = (P("shift", None, "row", "col", None), P("row", "col", None), P(), P(), P("shift"))
    return jax.shard_map(
        local,
        mesh=mesh,
        in_specs=placed,
        out_specs=(
            P("shift", None, "row", "col", None),
            P("shift", None),
            P("shift", None, "row", "col", None),
            P("shift", None),
        ),
        check_vma=False,
    )
```

```python
import jax
import jax.numpy as jnp
from jax import lax
from jax.sharding import PartitionSpec as P


def shifted(x, axis, by):
    peers = lax.axis_size(axis)
    pairs = [(i, i + by) for i in range(peers) if 0 <= i + by < peers]
    return lax.ppermute(x, axis, pairs)


def padded(x, sides, width):
    for axis, dim in sides:
        peers, length = (lax.axis_size(axis), x.shape[dim])
        up = [(i, (i + 1) % peers) for i in range(peers - 1)]
        down = [(j, i) for i, j in up]
        last = lax.slice_in_dim(x, length - width, length, axis=dim)
        leading = lax.slice_in_dim(x, 0, width, axis=dim)
        before = lax.ppermute(last, axis, up)
        after = lax.ppermute(leading, axis, down)
        x = jnp.concatenate([before, x, after], axis=dim)
    return x


def forward_z(values):
    return jnp.pad(values[..., 1:], ((0, 0), (0, 0), (0, 0), (0, 1))) - values


def backward_z(values):
    return values - jnp.pad(values[..., :-1], ((0, 0), (0, 0), (0, 0), (1, 0)))


def operator_block(padded_field, coupling, permittivity, shift_scalar):
    cells_x = padded_field.shape[2] - 2
    cells_y = padded_field.shape[3] - 2
    field_x = padded_field[:, 0]
    field_y = padded_field[:, 1]
    field_z = padded_field[:, 2]

    def corner_part(values):
        return values[:, : cells_x + 1, : cells_y + 1]

    def forward_x(values):
        return values[:, 1 : cells_x + 2, : cells_y + 1] - corner_part(values)

    def forward_y(values):
        return values[:, : cells_x + 1, 1 : cells_y + 2] - corner_part(values)

    def forward_dz(values):
        return forward_z(corner_part(values))

    curl_x = forward_y(field_z) - forward_dz(field_y)
    curl_y = forward_dz(field_x) - forward_x(field_z)
    curl_z = forward_x(field_y) - forward_y(field_x)
    weighted_x = coupling * curl_x
    weighted_y = coupling * curl_y
    weighted_z = coupling * curl_z

    def backward_x(values):
        return values[:, 1:, 1:] - values[:, :-1, 1:]

    def backward_y(values):
        return values[:, 1:, 1:] - values[:, 1:, :-1]

    def backward_dz(values):
        return backward_z(values[:, 1:, 1:])

    result_x = backward_y(weighted_z) - backward_dz(weighted_y)
    result_y = backward_dz(weighted_x) - backward_x(weighted_z)
    result_z = backward_x(weighted_y) - backward_y(weighted_x)
    interior = padded_field[:, :, 1 : cells_x + 1, 1 : cells_y + 1]
    stacked = jnp.stack([result_x, result_y, result_z], axis=1)
    return stacked - shift_scalar * permittivity * interior


def lookup(labels, table):
    regions = jnp.arange(table.shape[0], dtype=labels.dtype)
    chosen = jnp.where(labels[..., None] == regions, table, 0.0)
    return jnp.sum(chosen, axis=-1)


def butterfly_sum(x, axes):
    peers = 1
    for axis in axes:
        peers *= lax.axis_size(axis)
    step = 1
    while step < peers:
        x = x + lax.ppermute(x, axes, [(i, i ^ step) for i in range(peers)])
        step *= 2
    return x


def inner_products(left, right):
    return jnp.dot(
        left, right.T, precision=lax.Precision.HIGHEST, preferred_element_type=jnp.float32
    )


def apply_operator(padded_basis, coupling, permittivity, shift_scalar):
    columns = padded_basis.shape[0]
    blocks = padded_basis.reshape((columns // 16, 16) + padded_basis.shape[1:])

    def apply_block(column_block):
        return operator_block(column_block, coupling, permittivity, shift_scalar)

    images = lax.map(apply_block, blocks)
    return images.reshape((columns,) + images.shape[2:])


def factor_inverse(gram_matrix):
    lower_factor = jnp.linalg.cholesky(gram_matrix)
    inverse = lax.linalg.triangular_solve(
        lower_factor, jnp.eye(gram_matrix.shape[0], dtype=jnp.float32), left_side=True, lower=True
    )
    return (lower_factor.T, inverse)


def local(krylov_basis, regions, mu_table, eps_table, shift_value):
    columns = krylov_basis.shape[0]
    flattened = krylov_basis.reshape(columns, -1)
    total_rows = flattened.shape[1] * lax.axis_size("row") * lax.axis_size("col")
    cells_y = regions.shape[1]
    local_mu = lookup(regions, mu_table)
    from_lower_row = shifted(local_mu, "row", 1)
    from_lower_col = shifted(local_mu[:, cells_y - 1 :], "col", 1)
    corner_zero = jnp.zeros((1, 1, local_mu.shape[2]), jnp.float32)
    top_layer = jnp.concatenate([corner_zero, from_lower_row], axis=1)
    rest_layers = jnp.concatenate([from_lower_col, local_mu], axis=1)
    coupling = jnp.concatenate([top_layer, rest_layers], axis=0)
    permittivity = lookup(regions, eps_table)
    shift_scalar = shift_value[0]
    padded_basis = padded(krylov_basis, (("row", 2), ("col", 3)), 1)
    image_basis = operator_block(padded_basis, coupling, permittivity, shift_scalar)
    image_flat = image_basis.reshape(columns, -1)
    partial = jnp.stack(
        [
            inner_products(flattened, flattened) / total_rows,
            inner_products(flattened, image_flat) / total_rows,
        ]
    )
    gram_matrix, raw_proj = butterfly_sum(partial, ("row", "col"))
    upper_factor, inverse = factor_inverse(gram_matrix)
    orthonormal = jnp.dot(
        inverse, flattened, precision=lax.Precision.HIGHEST, preferred_element_type=jnp.float32
    ).reshape(krylov_basis.shape)
    applied = jnp.dot(
        inverse, image_flat, precision=lax.Precision.HIGHEST, preferred_element_type=jnp.float32
    ).reshape(krylov_basis.shape)
    half_proj = jnp.dot(
        inverse, raw_proj, precision=lax.Precision.HIGHEST, preferred_element_type=jnp.float32
    )
    projected = inner_products(half_proj, inverse)
    return (orthonormal, upper_factor, applied, projected)


def solution(mesh):
    placed = (P("shift", None, "row", "col", None), P("row", "col", None), P(), P(), P("shift"))
    return jax.shard_map(
        local,
        mesh=mesh,
        in_specs=placed,
        out_specs=(
            P("shift", None, "row", "col", None),
            P("shift", None),
            P("shift", None, "row", "col", None),
            P("shift", None),
        ),
        check_vma=False,
    )
```

```python
import jax
import jax.numpy as jnp
from jax import lax
from jax.sharding import PartitionSpec as P


def shifted(x, axis, by):
    peers = lax.axis_size(axis)
    pairs = [(i, i + by) for i in range(peers) if 0 <= i + by < peers]
    return lax.ppermute(x, axis, pairs)


def padded(x, sides, width):
    for axis, dim in sides:
        peers, length = (lax.axis_size(axis), x.shape[dim])
        up = [(i, (i + 1) % peers) for i in range(peers - 1)]
        down = [(j, i) for i, j in up]
        last = lax.slice_in_dim(x, length - width, length, axis=dim)
        leading = lax.slice_in_dim(x, 0, width, axis=dim)
        before = lax.ppermute(last, axis, up)
        after = lax.ppermute(leading, axis, down)
        x = jnp.concatenate([before, x, after], axis=dim)
    return x


def forward_z(values):
    return jnp.pad(values[..., 1:], ((0, 0), (0, 0), (0, 0), (0, 1))) - values


def backward_z(values):
    return values - jnp.pad(values[..., :-1], ((0, 0), (0, 0), (0, 0), (1, 0)))


def operator_block(padded_field, coupling, permittivity, shift_scalar):
    cells_x = padded_field.shape[2] - 2
    cells_y = padded_field.shape[3] - 2
    field_x = padded_field[:, 0]
    field_y = padded_field[:, 1]
    field_z = padded_field[:, 2]

    def corner_part(values):
        return values[:, : cells_x + 1, : cells_y + 1]

    def forward_x(values):
        return values[:, 1 : cells_x + 2, : cells_y + 1] - corner_part(values)

    def forward_y(values):
        return values[:, : cells_x + 1, 1 : cells_y + 2] - corner_part(values)

    def forward_dz(values):
        return forward_z(corner_part(values))

    curl_x = forward_y(field_z) - forward_dz(field_y)
    curl_y = forward_dz(field_x) - forward_x(field_z)
    curl_z = forward_x(field_y) - forward_y(field_x)
    weighted_x = coupling * curl_x
    weighted_y = coupling * curl_y
    weighted_z = coupling * curl_z

    def backward_x(values):
        return values[:, 1:, 1:] - values[:, :-1, 1:]

    def backward_y(values):
        return values[:, 1:, 1:] - values[:, 1:, :-1]

    def backward_dz(values):
        return backward_z(values[:, 1:, 1:])

    result_x = backward_y(weighted_z) - backward_dz(weighted_y)
    result_y = backward_dz(weighted_x) - backward_x(weighted_z)
    result_z = backward_x(weighted_y) - backward_y(weighted_x)
    interior = padded_field[:, :, 1 : cells_x + 1, 1 : cells_y + 1]
    stacked = jnp.stack([result_x, result_y, result_z], axis=1)
    return stacked - shift_scalar * permittivity * interior


def lookup(labels, table):
    regions = jnp.arange(table.shape[0], dtype=labels.dtype)
    chosen = jnp.where(labels[..., None] == regions, table, 0.0)
    return jnp.sum(chosen, axis=-1)


def butterfly_sum(x, axes):
    peers = 1
    for axis in axes:
        peers *= lax.axis_size(axis)
    step = 1
    while step < peers:
        x = x + lax.ppermute(x, axes, [(i, i ^ step) for i in range(peers)])
        step *= 2
    return x


def inner_products(left, right):
    return jnp.dot(
        left, right.T, precision=lax.Precision.HIGHEST, preferred_element_type=jnp.float32
    )


def apply_operator(padded_basis, coupling, permittivity, shift_scalar):
    columns = padded_basis.shape[0]
    blocks = padded_basis.reshape((columns // 16, 16) + padded_basis.shape[1:])

    def apply_block(column_block):
        return operator_block(column_block, coupling, permittivity, shift_scalar)

    images = lax.map(apply_block, blocks)
    return images.reshape((columns,) + images.shape[2:])


def factor_inverse(gram_matrix):
    lower_factor = jnp.linalg.cholesky(gram_matrix)
    inverse = lax.linalg.triangular_solve(
        lower_factor, jnp.eye(gram_matrix.shape[0], dtype=jnp.float32), left_side=True, lower=True
    )
    return (lower_factor.T, inverse)


def local(krylov_basis, regions, mu_table, eps_table, shift_value):
    columns = krylov_basis.shape[0]
    flattened = krylov_basis.reshape(columns, -1)
    total_rows = flattened.shape[1] * lax.axis_size("row") * lax.axis_size("col")
    cells_y = regions.shape[1]
    gram_matrix = butterfly_sum(inner_products(flattened, flattened) / total_rows, ("row", "col"))
    local_mu = lookup(regions, mu_table)
    from_lower_row = shifted(local_mu, "row", 1)
    from_lower_col = shifted(local_mu[:, cells_y - 1 :], "col", 1)
    corner_zero = jnp.zeros((1, 1, local_mu.shape[2]), jnp.float32)
    top_layer = jnp.concatenate([corner_zero, from_lower_row], axis=1)
    rest_layers = jnp.concatenate([from_lower_col, local_mu], axis=1)
    coupling = jnp.concatenate([top_layer, rest_layers], axis=0)
    permittivity = lookup(regions, eps_table)
    shift_scalar = shift_value[0]
    padded_basis = padded(krylov_basis, (("row", 2), ("col", 3)), 1)
    image_basis = operator_block(padded_basis, coupling, permittivity, shift_scalar)
    image_flat = image_basis.reshape(columns, -1)
    raw_proj = butterfly_sum(inner_products(flattened, image_flat) / total_rows, ("row", "col"))
    upper_factor, inverse = factor_inverse(gram_matrix)
    orthonormal = jnp.dot(
        inverse, flattened, precision=lax.Precision.HIGHEST, preferred_element_type=jnp.float32
    ).reshape(krylov_basis.shape)
    applied = jnp.dot(
        inverse, image_flat, precision=lax.Precision.HIGHEST, preferred_element_type=jnp.float32
    ).reshape(krylov_basis.shape)
    half_proj = jnp.dot(
        inverse, raw_proj, precision=lax.Precision.HIGHEST, preferred_element_type=jnp.float32
    )
    projected = inner_products(half_proj, inverse)
    return (orthonormal, upper_factor, applied, projected)


def solution(mesh):
    placed = (P("shift", None, "row", "col", None), P("row", "col", None), P(), P(), P("shift"))
    return jax.shard_map(
        local,
        mesh=mesh,
        in_specs=placed,
        out_specs=(
            P("shift", None, "row", "col", None),
            P("shift", None),
            P("shift", None, "row", "col", None),
            P("shift", None),
        ),
        check_vma=False,
    )
```

```python
import jax
import jax.numpy as jnp
from jax import lax
from jax.sharding import PartitionSpec as P


def shifted(x, axis, by):
    peers = lax.axis_size(axis)
    pairs = [(i, i + by) for i in range(peers) if 0 <= i + by < peers]
    return lax.ppermute(x, axis, pairs)


def padded(x, sides, width):
    for axis, dim, unused in sides:
        peers, length = (lax.axis_size(axis), x.shape[dim])
        up = [(i, (i + 1) % peers) for i in range(peers - 1)]
        down = [(j, i) for i, j in up]
        last = lax.slice_in_dim(x, length - width, length, axis=dim)
        leading = lax.slice_in_dim(x, 0, width, axis=dim)
        kept = [c for c in range(x.shape[1]) if c != unused]
        before = lax.ppermute(last, axis, up)
        sent = lax.ppermute(jnp.concatenate([leading[:, c : c + 1] for c in kept], axis=1), axis, down)
        parts = [sent[:, i : i + 1] for i in range(len(kept))]
        parts.insert(unused, jnp.zeros_like(parts[0]))
        after = jnp.concatenate(parts, axis=1)
        x = jnp.concatenate([before, x, after], axis=dim)
    return x


def forward_z(values):
    return jnp.pad(values[..., 1:], ((0, 0), (0, 0), (0, 0), (0, 1))) - values


def backward_z(values):
    return values - jnp.pad(values[..., :-1], ((0, 0), (0, 0), (0, 0), (1, 0)))


def operator_block(padded_field, coupling, permittivity, shift_scalar):
    cells_x = padded_field.shape[2] - 2
    cells_y = padded_field.shape[3] - 2
    field_x = padded_field[:, 0]
    field_y = padded_field[:, 1]
    field_z = padded_field[:, 2]

    def corner_part(values):
        return values[:, : cells_x + 1, : cells_y + 1]

    def forward_x(values):
        return values[:, 1 : cells_x + 2, : cells_y + 1] - corner_part(values)

    def forward_y(values):
        return values[:, : cells_x + 1, 1 : cells_y + 2] - corner_part(values)

    def forward_dz(values):
        return forward_z(corner_part(values))

    curl_x = forward_y(field_z) - forward_dz(field_y)
    curl_y = forward_dz(field_x) - forward_x(field_z)
    curl_z = forward_x(field_y) - forward_y(field_x)
    weighted_x = coupling * curl_x
    weighted_y = coupling * curl_y
    weighted_z = coupling * curl_z

    def backward_x(values):
        return values[:, 1:, 1:] - values[:, :-1, 1:]

    def backward_y(values):
        return values[:, 1:, 1:] - values[:, 1:, :-1]

    def backward_dz(values):
        return backward_z(values[:, 1:, 1:])

    result_x = backward_y(weighted_z) - backward_dz(weighted_y)
    result_y = backward_dz(weighted_x) - backward_x(weighted_z)
    result_z = backward_x(weighted_y) - backward_y(weighted_x)
    interior = padded_field[:, :, 1 : cells_x + 1, 1 : cells_y + 1]
    stacked = jnp.stack([result_x, result_y, result_z], axis=1)
    return stacked - shift_scalar * permittivity * interior


def lookup(labels, table):
    regions = jnp.arange(table.shape[0], dtype=labels.dtype)
    chosen = jnp.where(labels[..., None] == regions, table, 0.0)
    return jnp.sum(chosen, axis=-1)


def butterfly_sum(x, axes):
    peers = 1
    for axis in axes:
        peers *= lax.axis_size(axis)
    step = 1
    while step < peers:
        x = x + lax.ppermute(x, axes, [(i, i ^ step) for i in range(peers)])
        step *= 2
    return x


def inner_products(left, right):
    return jnp.dot(
        left, right.T, precision=lax.Precision.HIGHEST, preferred_element_type=jnp.float32
    )


def apply_operator(padded_basis, coupling, permittivity, shift_scalar):
    columns = padded_basis.shape[0]
    blocks = padded_basis.reshape((columns // 16, 16) + padded_basis.shape[1:])

    def apply_block(column_block):
        return operator_block(column_block, coupling, permittivity, shift_scalar)

    images = lax.map(apply_block, blocks)
    return images.reshape((columns,) + images.shape[2:])


def factor_inverse(gram_matrix):
    lower_factor = jnp.linalg.cholesky(gram_matrix)
    inverse = lax.linalg.triangular_solve(
        lower_factor, jnp.eye(gram_matrix.shape[0], dtype=jnp.float32), left_side=True, lower=True
    )
    return (lower_factor.T, inverse)


def local(krylov_basis, regions, mu_table, eps_table, shift_value):
    columns = krylov_basis.shape[0]
    flattened = krylov_basis.reshape(columns, -1)
    total_rows = flattened.shape[1] * lax.axis_size("row") * lax.axis_size("col")
    cells_y = regions.shape[1]
    local_mu = lookup(regions, mu_table)
    from_lower_row = shifted(local_mu, "row", 1)
    from_lower_col = shifted(local_mu[:, cells_y - 1 :], "col", 1)
    corner_zero = jnp.zeros((1, 1, local_mu.shape[2]), jnp.float32)
    top_layer = jnp.concatenate([corner_zero, from_lower_row], axis=1)
    rest_layers = jnp.concatenate([from_lower_col, local_mu], axis=1)
    coupling = jnp.concatenate([top_layer, rest_layers], axis=0)
    permittivity = lookup(regions, eps_table)
    shift_scalar = shift_value[0]
    padded_basis = padded(krylov_basis, (("row", 2, 0), ("col", 3, 1)), 1)
    image_basis = operator_block(padded_basis, coupling, permittivity, shift_scalar)
    image_flat = image_basis.reshape(columns, -1)
    partial = jnp.stack(
        [
            inner_products(flattened, flattened) / total_rows,
            inner_products(flattened, image_flat) / total_rows,
        ]
    )
    gram_matrix, raw_proj = butterfly_sum(partial, ("row", "col"))
    upper_factor, inverse = factor_inverse(gram_matrix)
    orthonormal = jnp.dot(
        inverse, flattened, precision=lax.Precision.HIGHEST, preferred_element_type=jnp.float32
    ).reshape(krylov_basis.shape)
    applied = jnp.dot(
        inverse, image_flat, precision=lax.Precision.HIGHEST, preferred_element_type=jnp.float32
    ).reshape(krylov_basis.shape)
    half_proj = jnp.dot(
        inverse, raw_proj, precision=lax.Precision.HIGHEST, preferred_element_type=jnp.float32
    )
    projected = inner_products(half_proj, inverse)
    return (orthonormal, upper_factor, applied, projected)


def solution(mesh):
    placed = (P("shift", None, "row", "col", None), P("row", "col", None), P(), P(), P("shift"))
    return jax.shard_map(
        local,
        mesh=mesh,
        in_specs=placed,
        out_specs=(
            P("shift", None, "row", "col", None),
            P("shift", None),
            P("shift", None, "row", "col", None),
            P("shift", None),
        ),
        check_vma=False,
    )
```

```python
import jax
import jax.numpy as jnp
from jax import lax
from jax.sharding import PartitionSpec as P


def shifted(x, axis, by):
    peers = lax.axis_size(axis)
    pairs = [(i, i + by) for i in range(peers) if 0 <= i + by < peers]
    return lax.ppermute(x, axis, pairs)


def padded(x, sides, width):
    riders = []
    for axis, dim, unused, rider in sides:
        peers, length = (lax.axis_size(axis), x.shape[dim])
        up = [(i, (i + 1) % peers) for i in range(peers - 1)]
        down = [(j, i) for i, j in up]
        last = lax.slice_in_dim(x, length - width, length, axis=dim)
        leading = lax.slice_in_dim(x, 0, width, axis=dim)
        kept = [c for c in range(x.shape[1]) if c != unused]
        carried = jnp.broadcast_to(rider, (1,) + last.shape[1:])
        received = lax.ppermute(jnp.concatenate([last, carried], axis=0), axis, up)
        before = received[: x.shape[0]]
        riders.append(received[x.shape[0] :])
        sent = lax.ppermute(jnp.concatenate([leading[:, c : c + 1] for c in kept], axis=1), axis, down)
        parts = [sent[:, i : i + 1] for i in range(len(kept))]
        parts.insert(unused, jnp.zeros_like(parts[0]))
        after = jnp.concatenate(parts, axis=1)
        x = jnp.concatenate([before, x, after], axis=dim)
    return x, riders


def forward_z(values):
    return jnp.pad(values[..., 1:], ((0, 0), (0, 0), (0, 0), (0, 1))) - values


def backward_z(values):
    return values - jnp.pad(values[..., :-1], ((0, 0), (0, 0), (0, 0), (1, 0)))


def operator_block(padded_field, coupling, permittivity, shift_scalar):
    cells_x = padded_field.shape[2] - 2
    cells_y = padded_field.shape[3] - 2
    field_x = padded_field[:, 0]
    field_y = padded_field[:, 1]
    field_z = padded_field[:, 2]

    def corner_part(values):
        return values[:, : cells_x + 1, : cells_y + 1]

    def forward_x(values):
        return values[:, 1 : cells_x + 2, : cells_y + 1] - corner_part(values)

    def forward_y(values):
        return values[:, : cells_x + 1, 1 : cells_y + 2] - corner_part(values)

    def forward_dz(values):
        return forward_z(corner_part(values))

    curl_x = forward_y(field_z) - forward_dz(field_y)
    curl_y = forward_dz(field_x) - forward_x(field_z)
    curl_z = forward_x(field_y) - forward_y(field_x)
    weighted_x = coupling * curl_x
    weighted_y = coupling * curl_y
    weighted_z = coupling * curl_z

    def backward_x(values):
        return values[:, 1:, 1:] - values[:, :-1, 1:]

    def backward_y(values):
        return values[:, 1:, 1:] - values[:, 1:, :-1]

    def backward_dz(values):
        return backward_z(values[:, 1:, 1:])

    result_x = backward_y(weighted_z) - backward_dz(weighted_y)
    result_y = backward_dz(weighted_x) - backward_x(weighted_z)
    result_z = backward_x(weighted_y) - backward_y(weighted_x)
    interior = padded_field[:, :, 1 : cells_x + 1, 1 : cells_y + 1]
    stacked = jnp.stack([result_x, result_y, result_z], axis=1)
    return stacked - shift_scalar * permittivity * interior


def lookup(labels, table):
    regions = jnp.arange(table.shape[0], dtype=labels.dtype)
    chosen = jnp.where(labels[..., None] == regions, table, 0.0)
    return jnp.sum(chosen, axis=-1)


def butterfly_sum(x, axes):
    peers = 1
    for axis in axes:
        peers *= lax.axis_size(axis)
    step = 1
    while step < peers:
        x = x + lax.ppermute(x, axes, [(i, i ^ step) for i in range(peers)])
        step *= 2
    return x


def inner_products(left, right):
    return jnp.dot(
        left, right.T, precision=lax.Precision.HIGHEST, preferred_element_type=jnp.float32
    )


def apply_operator(padded_basis, coupling, permittivity, shift_scalar):
    columns = padded_basis.shape[0]
    blocks = padded_basis.reshape((columns // 16, 16) + padded_basis.shape[1:])

    def apply_block(column_block):
        return operator_block(column_block, coupling, permittivity, shift_scalar)

    images = lax.map(apply_block, blocks)
    return images.reshape((columns,) + images.shape[2:])


def factor_inverse(gram_matrix):
    lower_factor = jnp.linalg.cholesky(gram_matrix)
    inverse = lax.linalg.triangular_solve(
        lower_factor, jnp.eye(gram_matrix.shape[0], dtype=jnp.float32), left_side=True, lower=True
    )
    return (lower_factor.T, inverse)


def local(krylov_basis, regions, mu_table, eps_table, shift_value):
    columns = krylov_basis.shape[0]
    flattened = krylov_basis.reshape(columns, -1)
    total_rows = flattened.shape[1] * lax.axis_size("row") * lax.axis_size("col")
    cells_y = regions.shape[1]
    local_mu = lookup(regions, mu_table)
    padded_basis, (row_rider, col_rider) = padded(
        krylov_basis,
        (("row", 2, 0, local_mu[None, None]), ("col", 3, 1, local_mu[None, None, :, cells_y - 1 :])),
        1,
    )
    from_lower_row = row_rider[0, 0]
    from_lower_col = col_rider[0, 0, :1]
    corner_zero = jnp.zeros((1, 1, local_mu.shape[2]), jnp.float32)
    top_layer = jnp.concatenate([corner_zero, from_lower_row], axis=1)
    rest_layers = jnp.concatenate([from_lower_col, local_mu], axis=1)
    coupling = jnp.concatenate([top_layer, rest_layers], axis=0)
    permittivity = lookup(regions, eps_table)
    shift_scalar = shift_value[0]
    image_basis = operator_block(padded_basis, coupling, permittivity, shift_scalar)
    image_flat = image_basis.reshape(columns, -1)
    partial = jnp.stack(
        [
            inner_products(flattened, flattened) / total_rows,
            inner_products(flattened, image_flat) / total_rows,
        ]
    )
    gram_matrix, raw_proj = butterfly_sum(partial, ("row", "col"))
    upper_factor, inverse = factor_inverse(gram_matrix)
    orthonormal = jnp.dot(
        inverse, flattened, precision=lax.Precision.HIGHEST, preferred_element_type=jnp.float32
    ).reshape(krylov_basis.shape)
    applied = jnp.dot(
        inverse, image_flat, precision=lax.Precision.HIGHEST, preferred_element_type=jnp.float32
    ).reshape(krylov_basis.shape)
    half_proj = jnp.dot(
        inverse, raw_proj, precision=lax.Precision.HIGHEST, preferred_element_type=jnp.float32
    )
    projected = inner_products(half_proj, inverse)
    return (orthonormal, upper_factor, applied, projected)


def solution(mesh):
    placed = (P("shift", None, "row", "col", None), P("row", "col", None), P(), P(), P("shift"))
    return jax.shard_map(
        local,
        mesh=mesh,
        in_specs=placed,
        out_specs=(
            P("shift", None, "row", "col", None),
            P("shift", None),
            P("shift", None, "row", "col", None),
            P("shift", None),
        ),
        check_vma=False,
    )
```

```python
import jax
import jax.numpy as jnp
from jax import lax
from jax.sharding import PartitionSpec as P


def shifted(x, axis, by):
    peers = lax.axis_size(axis)
    pairs = [(i, i + by) for i in range(peers) if 0 <= i + by < peers]
    return lax.ppermute(x, axis, pairs)


def padded(x, sides, width):
    riders = []
    for axis, dim, unused, rider in sides:
        peers, length = (lax.axis_size(axis), x.shape[dim])
        up = [(i, (i + 1) % peers) for i in range(peers - 1)]
        down = [(j, i) for i, j in up]
        last = lax.slice_in_dim(x, length - width, length, axis=dim)
        leading = lax.slice_in_dim(x, 0, width, axis=dim)
        kept = [c for c in range(x.shape[1]) if c != unused]
        carried = jnp.broadcast_to(rider, (1,) + last.shape[1:])
        received = lax.ppermute(jnp.concatenate([last, carried], axis=0), axis, up)
        before = received[: x.shape[0]]
        riders.append(received[x.shape[0] :])
        sent = lax.ppermute(jnp.concatenate([leading[:, c : c + 1] for c in kept], axis=1), axis, down)
        parts = [sent[:, i : i + 1] for i in range(len(kept))]
        parts.insert(unused, jnp.zeros_like(parts[0]))
        after = jnp.concatenate(parts, axis=1)
        x = jnp.concatenate([before, x, after], axis=dim)
    return x, riders


def forward_z(values):
    return jnp.pad(values[..., 1:], ((0, 0), (0, 0), (0, 0), (0, 1))) - values


def backward_z(values):
    return values - jnp.pad(values[..., :-1], ((0, 0), (0, 0), (0, 0), (1, 0)))


def operator_block(padded_field, coupling, permittivity, shift_scalar):
    cells_x = padded_field.shape[2] - 2
    cells_y = padded_field.shape[3] - 2
    field_x = padded_field[:, 0]
    field_y = padded_field[:, 1]
    field_z = padded_field[:, 2]

    def corner_part(values):
        return values[:, : cells_x + 1, : cells_y + 1]

    def forward_x(values):
        return values[:, 1 : cells_x + 2, : cells_y + 1] - corner_part(values)

    def forward_y(values):
        return values[:, : cells_x + 1, 1 : cells_y + 2] - corner_part(values)

    def forward_dz(values):
        return forward_z(corner_part(values))

    curl_x = forward_y(field_z) - forward_dz(field_y)
    curl_y = forward_dz(field_x) - forward_x(field_z)
    curl_z = forward_x(field_y) - forward_y(field_x)
    weighted_x = coupling * curl_x
    weighted_y = coupling * curl_y
    weighted_z = coupling * curl_z

    def backward_x(values):
        return values[:, 1:, 1:] - values[:, :-1, 1:]

    def backward_y(values):
        return values[:, 1:, 1:] - values[:, 1:, :-1]

    def backward_dz(values):
        return backward_z(values[:, 1:, 1:])

    result_x = backward_y(weighted_z) - backward_dz(weighted_y)
    result_y = backward_dz(weighted_x) - backward_x(weighted_z)
    result_z = backward_x(weighted_y) - backward_y(weighted_x)
    interior = padded_field[:, :, 1 : cells_x + 1, 1 : cells_y + 1]
    stacked = jnp.stack([result_x, result_y, result_z], axis=1)
    return stacked - shift_scalar * permittivity * interior


def lookup(labels, table):
    regions = jnp.arange(table.shape[0], dtype=labels.dtype)
    chosen = jnp.where(labels[..., None] == regions, table, 0.0)
    return jnp.sum(chosen, axis=-1)


def butterfly_sum(x, axes):
    peers = 1
    for axis in axes:
        peers *= lax.axis_size(axis)
    steps = [1 << b for b in range(peers.bit_length() - 1)]
    for step in steps[1:][::-1] + steps[:1]:
        x = x + lax.ppermute(x, axes, [(i, i ^ step) for i in range(peers)])
    return x


def inner_products(left, right):
    return jnp.dot(
        left, right.T, precision=lax.Precision.HIGHEST, preferred_element_type=jnp.float32
    )


def apply_operator(padded_basis, coupling, permittivity, shift_scalar):
    columns = padded_basis.shape[0]
    blocks = padded_basis.reshape((columns // 16, 16) + padded_basis.shape[1:])

    def apply_block(column_block):
        return operator_block(column_block, coupling, permittivity, shift_scalar)

    images = lax.map(apply_block, blocks)
    return images.reshape((columns,) + images.shape[2:])


def factor_inverse(gram_matrix):
    lower_factor = jnp.linalg.cholesky(gram_matrix)
    inverse = lax.linalg.triangular_solve(
        lower_factor, jnp.eye(gram_matrix.shape[0], dtype=jnp.float32), left_side=True, lower=True
    )
    return (lower_factor.T, inverse)


def local(krylov_basis, regions, mu_table, eps_table, shift_value):
    columns = krylov_basis.shape[0]
    flattened = krylov_basis.reshape(columns, -1)
    total_rows = flattened.shape[1] * lax.axis_size("row") * lax.axis_size("col")
    cells_y = regions.shape[1]
    local_mu = lookup(regions, mu_table)
    padded_basis, (row_rider, col_rider) = padded(
        krylov_basis,
        (("row", 2, 0, local_mu[None, None]), ("col", 3, 1, local_mu[None, None, :, cells_y - 1 :])),
        1,
    )
    from_lower_row = row_rider[0, 0]
    from_lower_col = col_rider[0, 0, :1]
    corner_zero = jnp.zeros((1, 1, local_mu.shape[2]), jnp.float32)
    top_layer = jnp.concatenate([corner_zero, from_lower_row], axis=1)
    rest_layers = jnp.concatenate([from_lower_col, local_mu], axis=1)
    coupling = jnp.concatenate([top_layer, rest_layers], axis=0)
    permittivity = lookup(regions, eps_table)
    shift_scalar = shift_value[0]
    image_basis = operator_block(padded_basis, coupling, permittivity, shift_scalar)
    image_flat = image_basis.reshape(columns, -1)
    partial = jnp.stack(
        [
            inner_products(flattened, flattened) / total_rows,
            inner_products(flattened, image_flat) / total_rows,
        ]
    )
    gram_matrix, raw_proj = butterfly_sum(partial, ("row", "col"))
    upper_factor, inverse = factor_inverse(gram_matrix)
    orthonormal = jnp.dot(
        inverse, flattened, precision=lax.Precision.HIGHEST, preferred_element_type=jnp.float32
    ).reshape(krylov_basis.shape)
    applied = jnp.dot(
        inverse, image_flat, precision=lax.Precision.HIGHEST, preferred_element_type=jnp.float32
    ).reshape(krylov_basis.shape)
    half_proj = jnp.dot(
        inverse, raw_proj, precision=lax.Precision.HIGHEST, preferred_element_type=jnp.float32
    )
    projected = inner_products(half_proj, inverse)
    return (orthonormal, upper_factor, applied, projected)


def solution(mesh):
    placed = (P("shift", None, "row", "col", None), P("row", "col", None), P(), P(), P("shift"))
    return jax.shard_map(
        local,
        mesh=mesh,
        in_specs=placed,
        out_specs=(
            P("shift", None, "row", "col", None),
            P("shift", None),
            P("shift", None, "row", "col", None),
            P("shift", None),
        ),
        check_vma=False,
    )
```
